32 devices in a mesh: band: 8 (over y, x, core), space: 4 (over z).
Axes of the slice: x: 2, y: 2, z: 4, core: 2. Of those that a mesh axis runs over, the one named last changes fastest.
Arguments:
- orbitals: bfloat16 [8, 192, 192, 192], P('band', 'space'), may hold values from -4 to 4
- occupations: float32 [8], P('band'), may hold values from 0.25 to 1
- shifts: float32 [8], P('band'), may hold values from 0.25 to 2
- perturbations: float32 [1, 192, 192, 192], P(None, 'space'), may hold values from -3 to 3
- local_potential: float32 [192, 192, 192], P('space'), may hold values from 0 to 1
Outputs:
- response_potential: float32 [1, 192, 192, 192], P(None, 'space', 'band')
The draws below stay inside these ranges and needn't reach their ends.
All inputs are finite; a program needn't handle non-finite values.
Results may differ from the reference program's by a relative error of at most 0.0003.
Values sent between devices are 32-bit elements; how exact they have to be, the bound alone decides.
No kernel may reach another device: no remote copies, remote signals or barrier semaphores. Data moves between devices by JAX's collectives and lax.ppermute only.
A program may use at most 320 MiB of HBM per device.

```python
import math
import jax
import jax.numpy as jnp
from jax import lax

NG = 192
PERT = 1
APPLY = 2
ORBS = 8


def draw_perturbations(key, part):
    field = 0.5 * jax.random.normal(key, (PERT, NG, NG, NG), jnp.float32)
    return jnp.clip(field, -3.0, 3.0)


def block_levels(key, dims, split, least, largest):
    gain = 1.0
    for position, parts in split:
        draws = jax.random.uniform(jax.random.fold_in(jax.random.fold_in(key, 6), position), (parts,), jnp.float32, least / len(split), largest / len(split))
        gain = gain * jnp.repeat(jnp.exp(draws), dims[position] // parts).reshape((-1,) + (1,) * (len(dims) - 1 - position))
    return gain


def bell_draw(stream_key, extent, width, bound, split=(), kind=jnp.bfloat16):
    level = block_levels(stream_key, extent, split, -0.22, 0.18) if split else 1.0
    drawn = jax.random.normal(stream_key, extent, jnp.float32) * width * level
    return jnp.minimum(jnp.maximum(drawn, -bound), bound).astype(kind)


def setup_inputs(seed: int = 0) -> dict:
    splits = jax.random.split(jax.random.key(seed), 6)
    return {
        "orbitals": bell_draw(splits[0], (ORBS, NG, NG, NG), 1.0, 4.0, ((0, 8), (1, 4))),
        "occupations": jnp.clip(jnp.exp(math.log(1.0) - 1.3862944 * jax.random.uniform(splits[1], (ORBS,), jnp.float32) ** block_levels(splits[1], (ORBS,), ((0, 8),), -0.2, 0.2)), 0.25, 1.0),
        "shifts": jnp.clip(jnp.exp(math.log(2.0) - 2.0794415 * jax.random.uniform(splits[2], (ORBS,), jnp.float32) ** block_levels(splits[2], (ORBS,), ((0, 8),), -0.2, 0.2)), 0.25, 2.0),
        "perturbations": draw_perturbations(jax.random.fold_in(splits[5], 71), 0),
        "local_potential": jnp.clip(1.0 * jax.random.uniform(splits[4], (NG, NG, NG), jnp.float32) ** block_levels(splits[4], (NG, NG, NG), ((0, 4),), -0.2, 0.2), 0.0, 1.0),
    }


COEFFS = (-205.0 / 72.0, 8.0 / 5.0, -1.0 / 5.0, 8.0 / 315.0, -1.0 / 560.0)

def laplacian(field):
    total = 3.0 * COEFFS[0] * field
    for offset in range(1, 5):
        for along in (1, 2, 3):
            total = total + COEFFS[offset] * (jnp.roll(field, offset, along) + jnp.roll(field, -offset, along))
    return total

def reference(orbitals, occupations, shifts, perturbations, local_potential):
    count = orbitals.shape[0]

    def accumulate(index, density):
        wave = orbitals[index].astype(jnp.float32)[None]
        shift_value = shifts[index]
        potential_plus = local_potential[None] + shift_value
        centre = shift_value + 5.5
        ratio_c = centre / 5.5
        source = -(perturbations * wave)
        iterate = jnp.zeros_like(source)
        residual = source
        direction = source / centre
        weight = 1.0 / ratio_c
        for repeat in range(APPLY):
            iterate = iterate + direction
            image = -0.5 * laplacian(direction) + potential_plus * direction
            residual = residual - image
            weight_new = 1.0 / (2.0 * ratio_c - weight)
            direction = weight_new * weight * direction + 2.0 * weight_new / 5.5 * residual
            weight = weight_new
        solved = iterate + direction
        return density + occupations[index] * wave * solved
    density = lax.fori_loop(0, count, accumulate, jnp.zeros(perturbations.shape, jnp.float32))
    density = density * (4.0 / count)
    freq = jnp.arange(NG, dtype=jnp.int32)
    folded_k = jnp.minimum(freq, NG - freq).astype(jnp.float32)
    squares = folded_k * folded_k
    kernel = 256.0 / jnp.sqrt(squares[:, None, None] + squares[None, :, None] + squares[None, None, :] + 1.0)
    spectrum = jnp.fft.fftn(density, axes=(1, 2, 3))
    return jnp.real(jnp.fft.ifftn(spectrum * kernel, axes=(1, 2, 3))).astype(jnp.float32)
```

```python
import math

import jax
import jax.numpy as jnp
import numpy as np
from jax import lax
from jax.experimental import pallas as pl
from jax.experimental.pallas import tpu as pltpu
from jax.sharding import PartitionSpec as P


LANES = 128
REACH = 4
COEFFS = (-205.0 / 72.0, 8.0 / 5.0, -1.0 / 5.0, 8.0 / 315.0, -1.0 / 560.0)
DENOM = 5040.0
MIB = 1 << 20
UNROLL = 4
F32 = jnp.float32
BF16 = jnp.bfloat16


def cas_np(rows, cols, count):
    prod = (np.asarray(rows, np.int64)[:, None] * np.asarray(cols, np.int64)[None, :]) % count
    ang = prod * (2.0 * math.pi / count)
    return (np.cos(ang) + np.sin(ang)).astype(np.float32)


def split_np(table):
    hi = table.astype(BF16)
    lo = (table - hi.astype(np.float32)).astype(BF16)
    return hi, lo


def circulant_np(count):
    mat = np.zeros((count, count), np.float64)
    for m in range(1, REACH + 1):
        for i in range(count):
            mat[i, (i + m) % count] += COEFFS[m] * DENOM
            mat[i, (i - m) % count] += COEFFS[m] * DENOM
    return np.round(mat).astype(np.float32).astype(BF16)


def partner(b, stage, bits):
    if stage == 0:
        return b ^ 1
    bit = stage if b % 2 == 0 else bits - stage
    return b ^ (1 << bit)


def block_orders(n_band):
    bits = n_band.bit_length() - 1
    held = {b: [b] for b in range(n_band)}
    for stage in range(bits - 1, -1, -1):
        held = {b: held[partner(b, stage, bits)] + held[b] for b in range(n_band)}
    return np.array([held[b] for b in range(n_band)], np.int32)


def split(values):
    hi = values.astype(BF16)
    lo = (values - hi.astype(F32)).astype(BF16)
    return hi, lo


def mm(a, b):
    return jnp.dot(a, b, preferred_element_type=F32)


def mm_nt(a, b):
    return lax.dot_general(a, b, (((1,), (1,)), ((), ())), preferred_element_type=F32)


def mm3(ah, al, b):
    bh, bl = split(b)
    return mm(ah, bh) + mm(ah, bl) + mm(al, bh)


def mm3_right(a, bh, bl):
    ah, al = split(a)
    return mm(ah, bh) + mm(al, bh) + mm(ah, bl)


def lap_yz(field, ccy_ref, cc_ref):
    hi, lo = split(field)
    stack = jnp.concatenate([hi, lo], axis=0)
    return mm(ccy_ref[...], stack) + mm(hi, cc_ref[...]) + mm(lo, cc_ref[...])


def spectra(pairs, before, begin, finish, ty_ref, tz_ref, ccy_ref, cc_ref, outs, lap, part, stack, freq):
    n = tz_ref.shape[0]
    half = n // 2
    wide = 2 * LANES
    for k in range(3):
        freq[:, :, k * wide + n:(k + 1) * wide] = jnp.zeros((UNROLL, n, wide - n), BF16)

    def sums(plane, slot):
        field, total = begin(plane, slice(0, n))
        hi, lo = split(field)
        lap[slot, :n, :] = hi
        lap[slot, n:, :] = lo
        part[slot] = total

    def stencil(slot):
        return mm(ccy_ref[...], lap[slot]) + mm(lap[slot, :n, :], cc_ref[...]) + mm(lap[slot, n:, :], cc_ref[...])

    def keep_rho(plane, slot, grad):
        rh, rl = split(finish(plane, part[slot], grad))
        for k, cells in enumerate((rh, rl, rh)):
            stack[slot, k * n:(k + 1) * n, :] = cells

    def keep_y(slot, values):
        eh, el = split(values)
        for k, cells in enumerate((eh, el, eh)):
            freq[slot, :, k * wide:k * wide + n] = cells

    def give(pair, odd, spec):
        cut = odd * (LANES // 2)
        for o, ref in enumerate(outs):
            cells = spec[o * half:(o + 1) * half]
            ref[pair, odd] = cells[:, :LANES]
            ref[pair, 2, :, cut:cut + LANES // 2] = cells[:, LANES:]

    def step(t, carry):
        before(t)
        for j in range(UNROLL):
            sums(UNROLL * t + j, j)
        grads = [stencil(j) for j in range(UNROLL)]
        for j in range(UNROLL):
            keep_rho(UNROLL * t + j, j, grads[j])
        for j in range(UNROLL):
            keep_y(j, mm(ty_ref[...], stack[j]))
        for j in range(UNROLL):
            give(UNROLL // 2 * t + j // 2, j % 2, mm_nt(tz_ref[...], freq[j]))
        return carry

    lax.fori_loop(0, 2 * pairs // UNROLL, step, 0)


def pack_plane(plane):
    n = plane.shape[0]
    tail = jnp.concatenate([plane[: n // 2, LANES:], plane[n // 2:, LANES:]], axis=1)
    return plane[:, :LANES], tail


def edges_kernel(share_ref, orb_hbm, pert_hbm, low, high, orb, pert, packed, sem):
    count_x, n = orb_hbm.shape[0], orb_hbm.shape[1]
    per_plane = n + n // 2
    whole = REACH * per_plane
    rows = whole // 2
    copies = []
    for side, start in enumerate((0, count_x - REACH)):
        for k, (src, dst) in enumerate(((orb_hbm, orb), (pert_hbm, pert))):
            c = pltpu.make_async_copy(src.at[pl.ds(start, REACH)], dst.at[side], sem.at[side, k])
            c.start()
            copies.append(c)
    for c in copies:
        c.wait()
    mine = pl.multiple_of(lax.rem(lax.axis_index("band"), 2) * rows, 8)
    for side, out in enumerate((low, high)):
        for j in range(REACH):
            main, tail = pack_plane(orb[side, j].astype(F32))
            out[pl.ds(j * per_plane, n), :] = main
            out[pl.ds(j * per_plane + n, n // 2), :] = tail
            main, tail = pack_plane(pert[side, j])
            packed[pl.ds(j * per_plane, n), :] = main
            packed[pl.ds(j * per_plane + n, n // 2), :] = tail
        out[pl.ds(whole, rows), :] = packed[pl.ds(mine, rows), :]


def order_rows(n_band, share_ref, base_ref, part, tz):
    width, n = base_ref.shape[1:]
    wide = 2 * LANES
    for p in range(n_band):
        part[0, p * width:(p + 1) * width, :] = base_ref[share_ref[lax.axis_index("band"), p]]
    hi, lo = split(part[0])
    for k, cells in enumerate((hi, hi, lo)):
        tz[:, k * wide:k * wide + n] = cells
        tz[:, k * wide + n:(k + 1) * wide] = jnp.zeros((n, wide - n), BF16)


C_SRC, C_A, C_B, C_S, C_D0, C_G, C_P, C_T = 0, 1, 2, 3, 8, 9, 10, 11


def first_apply(co, d0, idx, pot, ccy_ref, cc_ref):
    centre = d0[idx]
    total = (co[C_A] - co[C_B] * pot) * centre + co[C_S] * lap_yz(centre, ccy_ref, cc_ref)
    for m in range(1, REACH + 1):
        total = total + (co[C_S] * (COEFFS[m] * DENOM)) * (d0[idx + m] + d0[idx - m])
    return total


def second_begin(co, d0, d1, idx, at, pot):
    centre = d1[idx, at]
    total = co[C_D0] * d0 + (co[C_G] - co[C_P] * pot) * centre
    for m in range(1, REACH + 1):
        total = total + (co[C_T] * (COEFFS[m] * DENOM)) * (d1[idx + m, at] + d1[idx - m, at])
    return centre, total


def first_kernel(n_band, share_ref, co, orb_hbm, pert_hbm, pot_hbm, cc_ref, ccy_ref, ty_ref, base_ref,
                 d1_hbm, send_ref, keep_ref, orb, d0, pot, d1, tz, lap, part, stack, freq, sem, out_sem):
    count_x = orb.shape[0]
    groups = count_x // REACH
    arrays = ((orb_hbm, orb), (pert_hbm, d0), (pot_hbm, pot))

    def copy(k, g):
        src, dst = arrays[k]
        where = pl.ds(g * REACH, REACH)
        return pltpu.make_async_copy(src.at[where], dst.at[where], sem.at[k, g])

    def copy_out(g):
        where = pl.ds(g * REACH, REACH)
        return pltpu.make_async_copy(d1.at[where], d1_hbm.at[where], out_sem.at[g])

    def source(g):
        for k in range(3):
            copy(k, g).wait()
        for j in range(REACH):
            x = g * REACH + j
            d0[x] = co[C_SRC] * (d0[x] * orb[x].astype(F32))

    for g in range(groups):
        for k in range(3):
            copy(k, g).start()
    order_rows(n_band, share_ref, base_ref, part, tz)
    source(0)
    source(1)

    def step(g, carry):
        source(g)
        for j in range(REACH):
            x = (g - 1) * REACH + j
            d1[x] = first_apply(co, d0, x, pot[x], ccy_ref, cc_ref)
        copy_out(g - 1).start()
        return carry

    lax.fori_loop(2, groups, step, 0)
    lead = 2 * REACH

    def begin(p, at):
        return second_begin(co, d0[lead + p, at], d1, lead + p, at, pot[lead + p, at])

    def finish(p, total, grad):
        return orb[lead + p].astype(F32) * (total + co[C_T] * grad)

    spectra(send_ref.shape[0], lambda t: None, begin, finish, ty_ref, tz, ccy_ref, cc_ref, (send_ref, keep_ref),
            lap, part, stack, freq)

    def done(g, carry):
        copy_out(g).wait()
        return carry

    lax.fori_loop(1, groups - 1, done, 0)


def inner_kernel(n_band, start, share_ref, co, orb_hbm, pert_hbm, pot_hbm, d1_hbm, cc_ref, ccy_ref, ty_ref, base_ref,
                 send_ref, keep_ref, orb, pert, pot, d1, tz, lap, part, stack, freq, sem, first_sem):
    pairs = send_ref.shape[0]
    lead = 2 * REACH
    arrays = (
        (orb_hbm, orb, start, 0), (pert_hbm, pert, start, 0), (pot_hbm, pot, start, 0),
        (d1_hbm, d1, start + REACH, lead),
    )

    def copy(k, i):
        src, dst, at, to = arrays[k]
        return pltpu.make_async_copy(src.at[pl.ds(at + 2 * i, 2)], dst.at[pl.ds(to + 2 * i, 2)], sem.at[k, i])

    ahead = pltpu.make_async_copy(d1_hbm.at[pl.ds(start - REACH, lead)], d1.at[pl.ds(0, lead)], first_sem.at[0])
    ahead.start()
    for i in range(pairs):
        for k in range(4):
            copy(k, i).start()
    order_rows(n_band, share_ref, base_ref, part, tz)
    ahead.wait()

    def before(t):
        for i in range(UNROLL // 2):
            for k in range(4):
                copy(k, UNROLL // 2 * t + i).wait()

    def begin(p, at):
        d0 = co[C_SRC] * (pert[p, at] * orb[p, at].astype(F32))
        return second_begin(co, d0, d1, p + REACH, at, pot[p, at])

    def finish(p, total, grad):
        return orb[p].astype(F32) * (total + co[C_T] * grad)

    spectra(pairs, before, begin, finish, ty_ref, tz, ccy_ref, cc_ref, (send_ref, keep_ref), lap, part, stack, freq)


def boundary_kernel(n_band, side, share_ref, co, orb_hbm, pert_hbm, pot_hbm, d1_hbm, mine, other,
                    cc_ref, ccy_ref, ty_ref, base_ref, send_ref, keep_ref,
                    orb, psi, pert, pot, d0, d1, packed, tz, lap, part, stack, freq, sem):
    count_x, n = orb_hbm.shape[0], orb_hbm.shape[1]
    per_plane = n + n // 2
    whole = REACH * per_plane
    span = 3 * REACH
    own = (0, count_x - 2 * REACH)[side]
    at_own = (REACH, 0)[side]
    halo = (0, 2 * REACH)[side]
    d1_own = (REACH, count_x - 3 * REACH)[side]
    d1_at = (3 * REACH, 0)[side]
    far = (0, 3 * REACH)[side]
    copies = [
        pltpu.make_async_copy(src.at[pl.ds(own, 2 * REACH)], dst.at[pl.ds(at_own, 2 * REACH)], sem.at[k])
        for k, (src, dst) in enumerate(((orb_hbm, orb), (pert_hbm, pert), (pot_hbm, pot)))
    ]
    copies.append(pltpu.make_async_copy(
        d1_hbm.at[pl.ds(d1_own, 2 * REACH)], d1.at[pl.ds(d1_at, 2 * REACH)], sem.at[3]))
    for c in copies:
        c.start()
    order_rows(n_band, share_ref, base_ref, part, tz)
    zero = jnp.zeros((n, n), F32)
    core = lax.rem(lax.axis_index("band"), 2)
    rows = whole // 2
    packed[pl.ds(pl.multiple_of(core * rows, 8), rows), :] = mine[pl.ds(whole, rows), :]
    packed[pl.ds(pl.multiple_of((1 - core) * rows, 8), rows), :] = other[...]
    for j in range(REACH):
        for src, dst in ((mine, psi), (packed, d0)):
            base = j * per_plane
            tail = src[pl.ds(base + n, n // 2), :]
            dst[halo + j, :, :LANES] = src[pl.ds(base, n), :]
            dst[halo + j, : n // 2, LANES:] = tail[:, : n - LANES]
            dst[halo + j, n // 2:, LANES:] = tail[:, n - LANES:]
        pot[halo + j] = zero
        d0[halo + j] = co[C_SRC] * (d0[halo + j] * psi[halo + j])
    for j in range(2 * REACH):
        d1[far + j] = zero
    for c in copies:
        c.wait()

    def fill(i, carry):
        wave = orb[at_own + i].astype(F32)
        psi[at_own + i] = wave
        d0[at_own + i] = co[C_SRC] * (pert[at_own + i] * wave)
        return carry

    lax.fori_loop(0, 2 * REACH, fill, 0)
    for j in range(REACH):
        d1[2 * REACH + j] = first_apply(co, d0, REACH + j, pot[REACH + j], ccy_ref, cc_ref)
    for j in range(REACH):
        d0[halo + j] = zero

    def begin(p, at):
        return second_begin(co, d0[p, at], d1, p + REACH, at, pot[p, at])

    def finish(p, total, grad):
        return psi[p] * (total + co[C_T] * grad)

    spectra(span // 2, lambda t: None, begin, finish, ty_ref, tz, ccy_ref, cc_ref, (send_ref, keep_ref),
            lap, part, stack, freq)


def pack_kernel(n_space, terms, share_ref, *refs):
    count = sum(terms)
    outs, cells = refs[count:-1], refs[-1]
    piece, size = outs[0].shape[0], outs[0].shape[1]
    width = refs[0].shape[2]
    half = width // 2
    slab = lax.axis_index("space")
    chunks = [refs[sum(terms[:c]):sum(terms[:c + 1])] for c in range(len(terms))]
    total = 2 * sum(chunk[0].shape[0] for chunk in chunks)
    if total < size or piece * n_space > 3 * half:
        cells[...] = jnp.zeros_like(cells)
    low = lax.broadcasted_iota(jnp.int32, (half, LANES), 1) < LANES // 2
    x = 0
    for chunk in chunks:
        for i in range(chunk[0].shape[0]):
            for j in range(2):
                cells[pl.ds(x + j, width, stride=size), :] = sum(ref[i, j] for ref in chunk[1:]) + chunk[0][i, j]
            tail = sum(ref[i, 2] for ref in chunk[1:]) + chunk[0][i, 2]
            a, b = tail[:half], tail[half:]
            cells[pl.ds(width * size + x, half, stride=size), :] = jnp.where(low, a, pltpu.roll(b, LANES // 2, 1))
            cells[pl.ds(width * size + x + 1, half, stride=size), :] = jnp.where(low, pltpu.roll(a, LANES // 2, 1), b)
            x += 2
    for k in range(n_space):
        dest = lax.rem(slab + k, n_space)
        for r in range(piece):
            where = pl.multiple_of((dest * piece + r) * size, 8)
            outs[k][r] = cells[pl.ds(where, size), :]


def x_kernel(n_space, batches, share_ref, *refs):
    ins = refs[:batches * n_space]
    ah_ref, al_ref, bh_ref, bl_ref, mul_ref = refs[batches * n_space:batches * n_space + 5]
    outs = refs[batches * n_space + 5:-2]
    cells, back = refs[-2:]
    slab = lax.axis_index("space")
    rows, size_out = outs[0].shape[0], outs[0].shape[1]
    parts = len(outs) // n_space
    total = sum(ins[i * n_space].shape[1] for i in range(batches))
    for k in range(n_space):
        at = lax.rem(slab - k + n_space, n_space) * total
        for i in range(batches):
            ref = ins[i * n_space + k]
            size = ref.shape[1]
            for r in range(rows):
                cells[pl.ds(pl.multiple_of(at, 8), size), r * LANES:(r + 1) * LANES] = ref[r]
            at = at + size
    spec = mm3(ah_ref[...], al_ref[...], cells[...]) * mul_ref[...]
    back[...] = mm3(bh_ref[...], bl_ref[...], spec)
    for k in range(n_space):
        for h in range(parts):
            at = pl.multiple_of((lax.rem(slab + k, n_space) * parts + h) * size_out, 8)
            for r in range(rows):
                outs[h * n_space + k][r] = back[pl.ds(at, size_out), r * LANES:(r + 1) * LANES]


def y_kernel(n_space, width, share_ref, *refs):
    ins = refs[:n_space]
    wh_ref, wl_ref = refs[n_space:n_space + 2]
    outs = refs[n_space + 2:-4]
    cells, rows_ref, prod, mixed = refs[-4:]
    piece, count_x = ins[0].shape[0], ins[0].shape[1]
    n_band = len(outs)
    half = width // 2
    per_tile = LANES // width
    tiles = outs[0].shape[0] // width
    me, slab = lax.axis_index("band"), lax.axis_index("space")
    for k in range(n_space):
        src = lax.rem(slab - k + n_space, n_space)
        for r in range(piece):
            where = pl.multiple_of((src * piece + r) * count_x, 8)
            cells[pl.ds(where, count_x), :] = ins[k][r]
    for i in range(per_tile):
        for t in range(tiles):
            x = t * per_tile + i
            at = (i * tiles + t) * width
            if x >= count_x:
                rows_ref[pl.ds(at, width), :] = jnp.zeros((width, 2 * LANES), F32)
                continue
            tail = cells[pl.ds(width * count_x + x, half, stride=count_x), :]
            rows_ref[pl.ds(at, width), :LANES] = cells[pl.ds(x, width, stride=count_x), :]
            rows_ref[pl.ds(at, half), LANES:] = tail
            rows_ref[pl.ds(at + half, half), LANES:] = pltpu.roll(tail, LANES // 2, 1)
    prod[...] = mm3_right(rows_ref[...], wh_ref[...], wl_ref[...])
    size = tiles * width
    lane = lax.broadcasted_iota(jnp.int32, (size, LANES), 1)
    for b in range(n_band):
        tile, spot = divmod(b, per_tile)
        acc = jnp.zeros((size, LANES), F32)
        for i in range(per_tile):
            part = prod[pl.ds(i * size, size), tile * LANES:(tile + 1) * LANES]
            shift = (i - spot) * width % LANES
            if shift:
                part = pltpu.roll(part, shift, 1)
            acc = jnp.where((lane >= i * width) & (lane < (i + 1) * width), part, acc)
        mixed[b ^ me] = acc
    for p in range(n_band):
        outs[p][...] = mixed[p]


def z_kernel(n_band, share_ref, *refs):
    th_ref, tl_ref, out_ref, stack = refs[-4:]
    ins = refs[:-4]
    parts = len(ins) // n_band
    count_x, width = out_ref.shape[0], out_ref.shape[1]
    size = count_x // parts
    per_tile = LANES // width
    tiles = ins[0].shape[0] // width
    for h in range(parts):
        for p in range(n_band):
            block = lax.axis_index("band") ^ p
            for t in range(tiles):
                stack[h * tiles + t, block] = ins[h * n_band + p][t * width:(t + 1) * width]
    for h in range(parts):
        for t in range(tiles):
            cells = stack[h * tiles + t].reshape(n_band * width, LANES)
            plane = mm3_right(cells.T, th_ref[...], tl_ref[...])
            for i in range(per_tile):
                x = t * per_tile + i
                if x < size:
                    out_ref[h * size + x] = plane[i * width:(i + 1) * width]


def shape_of(*dims, dtype=F32):
    return jax.ShapeDtypeStruct(dims, dtype)


def shift_perm(count, k):
    return [(i, (i + k) % count) for i in range(count)]


def coefficients(shift, occupation, total_orbitals):
    delta = 5.5
    theta = shift + delta
    ratio = theta / delta
    w0 = 1.0 / ratio
    w1 = 1.0 / (2.0 * ratio - w0)
    w2 = 1.0 / (2.0 * ratio - w1)
    b1 = 2.0 * w1 / delta
    b2 = 2.0 * w2 / delta
    weight = occupation * (4.0 / total_orbitals)
    centre = -0.5 * 3.0 * COEFFS[0]
    co = [jnp.zeros_like(shift)] * 16
    co[C_SRC] = -1.0 / theta
    co[C_A] = w1 * w0 + b1 * theta - b1 * (shift + centre)
    co[C_B] = b1
    co[C_S] = 0.5 * b1 / DENOM
    co[C_D0] = weight * (1.0 - w2 * w0)
    co[C_G] = weight * (1.0 + w2 * w1 + w2 / w1 - b2 * (shift + centre))
    co[C_P] = weight * b2
    co[C_T] = weight * 0.5 * b2 / DENOM
    return jnp.stack(co)


def chunk_sizes(groups):
    first = -(-groups // 2)
    return [first, groups - first]


def ceil8(count):
    return -(-count // 8) * 8


def program_on_device(orbitals, occupations, shifts, perturbations, local_potential):
    count_x, n = orbitals.shape[1], orbitals.shape[2]
    n_band, n_space = lax.axis_size("band"), lax.axis_size("space")
    bits = n_band.bit_length() - 1
    assert orbitals.shape[0] == 1 and perturbations.shape[0] == 1 and n_band == 1 << bits
    assert 2 * (n - LANES) == LANES and count_x % 8 == 0 and count_x >= 5 * REACH
    band, slab = lax.axis_index("band"), lax.axis_index("space")
    orders = block_orders(n_band)
    share = jnp.asarray(orders)
    orb, pert, pot = orbitals[0], perturbations[0], local_potential
    width = n // n_band
    half = width // 2
    per_plane = n + n // 2
    wide = 2 * LANES
    smem = pl.BlockSpec(memory_space=pltpu.SMEM)
    vmem = pl.BlockSpec(memory_space=pltpu.VMEM)
    anywhere = pl.BlockSpec(memory_space=pl.ANY)
    dma = pltpu.SemaphoreType.DMA
    co = coefficients(shifts[0], occupations[0], n_band * orbitals.shape[0])

    base = cas_np(range(n), range(n), n)
    base_h, base_l = split_np(base)
    ring = circulant_np(n)
    ring_y = np.concatenate([ring, ring], axis=1)
    ty = np.concatenate([base_h, base_h, base_l], axis=1)
    whole = REACH * per_plane
    low, high = pl.pallas_call(
        edges_kernel,
        out_shape=[shape_of(whole + whole // 2, LANES)] * 2,
        in_specs=[smem, anywhere, anywhere],
        out_specs=[vmem] * 2,
        scratch_shapes=[
            pltpu.VMEM((2, REACH, n, n), BF16), pltpu.VMEM((2, REACH, n, n), F32),
            pltpu.VMEM((whole, LANES), F32), dma((2, 2)),
        ],
        name="edges", compiler_params=pltpu.CompilerParams(vmem_limit_bytes=12 * MIB),
    )(share, orb, pert)
    cores = [(b, b ^ 1) for b in range(n_band)]
    halos = []
    for cells, k in ((high, 1), (low, n_space - 1)):
        mine = lax.ppermute(cells, "space", shift_perm(n_space, k))
        other = lax.ppermute(mine[whole:], "band", cores)
        halos.append((mine, other))

    tables = (jnp.asarray(ring), jnp.asarray(ring_y), jnp.asarray(ty), jnp.asarray(base.reshape(n_band, width, n)))
    table_specs = [vmem] * 4

    def halves(pairs):
        return [shape_of(pairs, 3, n // 2, LANES)] * 2

    def stages():
        return [
            pltpu.VMEM((n, 3 * wide), BF16), pltpu.VMEM((UNROLL, 2 * n, n), BF16), pltpu.VMEM((UNROLL, n, n), F32),
            pltpu.VMEM((UNROLL, 3 * n, n), BF16), pltpu.VMEM((UNROLL, n, 3 * wide), BF16),
        ]

    chunks = chunk_sizes(count_x // REACH - 4)
    size_a = chunks[0] * REACH
    d1, *sent_a = pl.pallas_call(
        lambda *refs: first_kernel(n_band, *refs),
        out_shape=[shape_of(count_x, n, n)] + halves(size_a // 2),
        in_specs=[smem, smem] + [anywhere] * 3 + table_specs,
        out_specs=[anywhere, vmem, vmem],
        scratch_shapes=[
            pltpu.VMEM((count_x, n, n), BF16), pltpu.VMEM((count_x, n, n), F32),
            pltpu.VMEM((count_x, n, n), F32), pltpu.VMEM((count_x, n, n), F32), *stages(),
            dma((3, count_x // REACH)), dma((count_x // REACH,)),
        ],
        name="first_a", compiler_params=pltpu.CompilerParams(vmem_limit_bytes=52 * MIB),
    )(share, co, orb, pert, pot, *tables)

    def inner(start, count):
        return pl.pallas_call(
            lambda *refs: inner_kernel(n_band, start, *refs),
            out_shape=halves(count // 2),
            in_specs=[smem, smem] + [anywhere] * 4 + table_specs,
            out_specs=[vmem, vmem],
            scratch_shapes=[
                pltpu.VMEM((count, n, n), BF16), pltpu.VMEM((count, n, n), F32), pltpu.VMEM((count, n, n), F32),
                pltpu.VMEM((count + 2 * REACH, n, n), F32), *stages(), dma((4, count // 2)), dma((1,)),
            ],
            compiler_params=pltpu.CompilerParams(vmem_limit_bytes=28 * MIB),
        )(share, co, orb, pert, pot, d1, *tables)

    span = 3 * REACH

    def outer(side, halo):
        return pl.pallas_call(
            lambda *refs: boundary_kernel(n_band, side, *refs),
            out_shape=halves(span // 2),
            in_specs=[smem, smem] + [anywhere] * 4 + [vmem] * 2 + table_specs,
            out_specs=[vmem, vmem],
            scratch_shapes=[
                pltpu.VMEM((span, n, n), BF16), pltpu.VMEM((span, n, n), F32), pltpu.VMEM((span, n, n), F32),
                pltpu.VMEM((span, n, n), F32), pltpu.VMEM((span, n, n), F32), pltpu.VMEM((5 * REACH, n, n), F32),
                pltpu.VMEM((whole, LANES), F32), *stages(), dma((4,)),
            ],
            compiler_params=pltpu.CompilerParams(vmem_limit_bytes=28 * MIB),
        )(share, co, orb, pert, pot, d1, *halo, *tables)

    def halving(send, keep):
        for stage in range(bits):
            perm = [(b, partner(b, stage, bits)) for b in range(n_band)]
            got = lax.ppermute(send, "band", perm)
            if stage < bits - 1:
                cut = keep.shape[2] // 2
                send, keep = keep[:, :, :cut] + got[:, :, :cut], keep[:, :, cut:] + got[:, :, cut:]
        return [keep, got]

    def direct(send, keep):
        perm = [(b, partner(b, 0, bits)) for b in range(n_band)]
        got = lax.ppermute(send, "band", perm)
        blocks = []
        for m in range(n_band // 2):
            rows = slice(m * width, (m + 1) * width)
            block = keep[:, :, rows] + got[:, :, rows]
            if m < n_band // 2 - 1:
                perm = [(b, int(orders[b, n_band // 2 + m])) for b in range(n_band)]
                block = lax.ppermute(block, "band", perm)
            blocks.append(block)
        return blocks

    piece = -(-3 * half // n_space)

    def to_columns(chunks):
        size = ceil8(2 * sum(chunk[0].shape[0] for chunk in chunks))
        blocks = pl.pallas_call(
            lambda *refs: pack_kernel(n_space, [len(chunk) for chunk in chunks], *refs),
            out_shape=[shape_of(piece, size, LANES)] * n_space,
            in_specs=[smem] + [vmem] * sum(len(chunk) for chunk in chunks),
            out_specs=[vmem] * n_space,
            scratch_shapes=[pltpu.VMEM((piece * n_space * size, LANES), F32)],
            compiler_params=pltpu.CompilerParams(vmem_limit_bytes=12 * MIB),
        )(share, *(ref for chunk in chunks for ref in chunk))
        return [lax.ppermute(blocks[k], "space", shift_perm(n_space, k)) if k else blocks[0] for k in range(n_space)]

    inside = np.arange(2 * REACH, count_x - 2 * REACH)
    planes = {
        "a": inside[:size_a],
        "b": inside[size_a:],
        "p": np.arange(-REACH, 2 * REACH),
        "q": np.arange(count_x - 2 * REACH, count_x + REACH),
    }
    sums = [
        direct(*sent_a),
        direct(*inner(2 * REACH + size_a, chunks[1] * REACH)),
        halving(*outer(0, halos[0])),
        halving(*outer(1, halos[1])),
    ]
    batches = (("a", "b"), ("p", "q"))
    at = dict(zip(planes, sums))
    received = [to_columns([at[name] for name in names]) for names in batches]

    a_parts = []
    for s in range(n_space):
        for names in batches:
            at = np.concatenate([planes[name] for name in names])
            block = base[:, (s * count_x + at) % n]
            a_parts.append(np.pad(block, ((0, 0), (0, ceil8(len(at)) - len(at)))))
    a_h, a_l = split_np(np.concatenate(a_parts, axis=1))

    def folded(values):
        return jnp.minimum(values, n - values).astype(F32)

    row = slab * piece + jnp.arange(piece, dtype=jnp.int32)[:, None]
    lane = jnp.arange(LANES, dtype=jnp.int32)[None, :]
    is_tail = row >= width
    ky = jnp.where(is_tail, LANES + lane % (LANES // 2), lane)
    kz_in = jnp.where(is_tail, row - width + jnp.where(lane < LANES // 2, 0, half), row)
    kz = jnp.clip(band * width + kz_in, 0, n)
    squares = (folded(ky) ** 2 + folded(kz) ** 2).reshape(1, piece * LANES)
    kx = folded(jnp.arange(n, dtype=jnp.int32))
    multiplier = (256.0 / float(n) ** 3) / jnp.sqrt(squares + (kx ** 2)[:, None] + 1.0)

    n_parts = 1
    part_x = count_x // n_parts
    base_h, base_l = jnp.asarray(base_h), jnp.asarray(base_l)
    backs = pl.pallas_call(
        lambda *refs: x_kernel(n_space, len(received), *refs),
        out_shape=[shape_of(piece, part_x, LANES)] * (n_space * n_parts),
        in_specs=[smem] + [vmem] * (len(received) * n_space + 5),
        out_specs=[vmem] * (n_space * n_parts),
        scratch_shapes=[
            pltpu.VMEM((a_h.shape[1], piece * LANES), F32), pltpu.VMEM((n, piece * LANES), F32),
        ],
        name="along_x", compiler_params=pltpu.CompilerParams(vmem_limit_bytes=20 * MIB),
    )(share, *(ref for blocks in received for ref in blocks), jnp.asarray(a_h), jnp.asarray(a_l), base_h, base_l, multiplier)
    per_tile = LANES // width
    tiles = -(-part_x // per_tile)
    y_tiles = -(-n_band // per_tile)
    w_table = np.zeros((wide, y_tiles * LANES), np.float32)
    for b in range(n_band):
        t, spot = divmod(b, per_tile)
        w_table[:n, t * LANES + spot * width:t * LANES + (spot + 1) * width] = base[:, b * width:(b + 1) * width]
    w_h, w_l = split_np(w_table)
    rows_y = per_tile * tiles * width
    pieces = []
    for h in range(n_parts):
        blocks = backs[h * n_space:(h + 1) * n_space]
        slabs = [lax.ppermute(blocks[k], "space", shift_perm(n_space, k)) if k else blocks[0] for k in range(n_space)]
        by_rows = pl.pallas_call(
            lambda *refs: y_kernel(n_space, width, *refs),
            out_shape=[shape_of(tiles * width, LANES)] * n_band,
            in_specs=[smem] + [vmem] * (n_space + 2),
            out_specs=[vmem] * n_band,
            scratch_shapes=[
                pltpu.VMEM((piece * n_space * part_x, LANES), F32),
                pltpu.VMEM((rows_y, wide), F32),
                pltpu.VMEM((rows_y, y_tiles * LANES), F32),
                pltpu.VMEM((n_band, tiles * width, LANES), F32),
            ],
            compiler_params=pltpu.CompilerParams(vmem_limit_bytes=24 * MIB),
        )(share, *slabs, jnp.asarray(w_h), jnp.asarray(w_l))
        pieces += [
            lax.ppermute(by_rows[p], "band", [(b, b ^ p) for b in range(n_band)])
            if p else by_rows[0]
            for p in range(n_band)
        ]

    out = pl.pallas_call(
        lambda *refs: z_kernel(n_band, *refs),
        out_shape=shape_of(count_x, width, n),
        in_specs=[smem] + [vmem] * (n_parts * n_band + 2),
        out_specs=vmem,
        scratch_shapes=[pltpu.VMEM((n_parts * tiles, n_band, width, LANES), F32)],
        name="along_z", compiler_params=pltpu.CompilerParams(vmem_limit_bytes=16 * MIB),
    )(share, *pieces, base_h, base_l)
    return out[None]


def solution(mesh):
    in_specs = (
        P("band", "space", None, None),
        P("band"),
        P("band"),
        P(None, "space", None, None),
        P("space", None, None),
    )
    out_specs = P(None, "space", "band", None)
    return jax.shard_map(program_on_device, mesh=mesh, in_specs=in_specs, out_specs=out_specs, check_vma=False)
```

```python
import math

import jax
import jax.numpy as jnp
import numpy as np
from jax import lax
from jax.experimental import pallas as pl
from jax.experimental.pallas import tpu as pltpu
from jax.sharding import PartitionSpec as P


LANES = 128
REACH = 4
COEFFS = (-205.0 / 72.0, 8.0 / 5.0, -1.0 / 5.0, 8.0 / 315.0, -1.0 / 560.0)
DENOM = 5040.0
MIB = 1 << 20
MOST = 119 * MIB // 2
UNROLL = 4
F32 = jnp.float32
BF16 = jnp.bfloat16


def cas_np(rows, cols, count):
    prod = (np.asarray(rows, np.int64)[:, None] * np.asarray(cols, np.int64)[None, :]) % count
    ang = prod * (2.0 * math.pi / count)
    return (np.cos(ang) + np.sin(ang)).astype(np.float32)


def split_np(table):
    hi = table.astype(BF16)
    lo = (table - hi.astype(np.float32)).astype(BF16)
    return hi, lo


def circulant_np(count):
    mat = np.zeros((count, count), np.float64)
    for m in range(1, REACH + 1):
        for i in range(count):
            mat[i, (i + m) % count] += COEFFS[m] * DENOM
            mat[i, (i - m) % count] += COEFFS[m] * DENOM
    return np.round(mat).astype(np.float32).astype(BF16)


def partner(b, stage, bits):
    if stage == 0:
        return b ^ 1
    bit = stage if b % 2 == 0 else bits - stage
    return b ^ (1 << bit)


def block_orders(n_band):
    bits = n_band.bit_length() - 1
    held = {b: [b] for b in range(n_band)}
    for stage in range(bits - 1, -1, -1):
        held = {b: held[partner(b, stage, bits)] + held[b] for b in range(n_band)}
    return np.array([held[b] for b in range(n_band)], np.int32)


def split(values):
    hi = values.astype(BF16)
    lo = (values - hi.astype(F32)).astype(BF16)
    return hi, lo


def mm(a, b):
    return jnp.dot(a, b, preferred_element_type=F32)


def mm_nt(a, b):
    return lax.dot_general(a, b, (((1,), (1,)), ((), ())), preferred_element_type=F32)


def mm3(ah, al, b):
    bh, bl = split(b)
    return mm(ah, bh) + mm(ah, bl) + mm(al, bh)


def mm3_right(a, bh, bl):
    ah, al = split(a)
    return mm(ah, bh) + mm(al, bh) + mm(ah, bl)


def lap_yz(field, ccy_ref, cc_ref):
    hi, lo = split(field)
    stack = jnp.concatenate([hi, lo], axis=0)
    return mm(ccy_ref[...], stack) + mm(hi, cc_ref[...]) + mm(lo, cc_ref[...])


def spectra(pairs, before, begin, finish, ty_ref, tz_ref, ccy_ref, cc_ref, outs, lap, part, stack, freq):
    n = tz_ref.shape[0]
    half = n // 2
    wide = 2 * LANES
    for k in range(3):
        freq[:, :, k * wide + n:(k + 1) * wide] = jnp.zeros((UNROLL, n, wide - n), BF16)

    def sums(plane, slot):
        field, total = begin(plane, slice(0, n))
        hi, lo = split(field)
        lap[slot, :n, :] = hi
        lap[slot, n:, :] = lo
        part[slot] = total

    def stencil(slot):
        return mm(ccy_ref[...], lap[slot]) + mm(lap[slot, :n, :], cc_ref[...]) + mm(lap[slot, n:, :], cc_ref[...])

    def keep_rho(plane, slot, grad):
        rh, rl = split(finish(plane, part[slot], grad))
        for k, cells in enumerate((rh, rl, rh)):
            stack[slot, k * n:(k + 1) * n, :] = cells

    def keep_y(slot, values):
        eh, el = split(values)
        for k, cells in enumerate((eh, el, eh)):
            freq[slot, :, k * wide:k * wide + n] = cells

    def give(pair, odd, spec):
        cut = odd * (LANES // 2)
        for o, ref in enumerate(outs):
            cells = spec[o * half:(o + 1) * half]
            ref[pair, odd] = cells[:, :LANES]
            ref[pair, 2, :, cut:cut + LANES // 2] = cells[:, LANES:]

    def step(t, carry):
        before(t)
        for j in range(UNROLL):
            sums(UNROLL * t + j, j)
        grads = [stencil(j) for j in range(UNROLL)]
        for j in range(UNROLL):
            keep_rho(UNROLL * t + j, j, grads[j])
        for j in range(UNROLL):
            keep_y(j, mm(ty_ref[...], stack[j]))
        for j in range(UNROLL):
            give(UNROLL // 2 * t + j // 2, j % 2, mm_nt(tz_ref[...], freq[j]))
        return carry

    lax.fori_loop(0, 2 * pairs // UNROLL, step, 0)


def pack_plane(plane):
    n = plane.shape[0]
    tail = jnp.concatenate([plane[: n // 2, LANES:], plane[n // 2:, LANES:]], axis=1)
    return plane[:, :LANES], tail


def edges_kernel(share_ref, orb_hbm, pert_hbm, low, high, orb, pert, packed, sem):
    count_x, n = orb_hbm.shape[0], orb_hbm.shape[1]
    per_plane = n + n // 2
    whole = REACH * per_plane
    rows = whole // 2
    copies = []
    for side, start in enumerate((0, count_x - REACH)):
        for k, (src, dst) in enumerate(((orb_hbm, orb), (pert_hbm, pert))):
            c = pltpu.make_async_copy(src.at[pl.ds(start, REACH)], dst.at[side], sem.at[side, k])
            c.start()
            copies.append(c)
    for c in copies:
        c.wait()
    mine = pl.multiple_of(lax.rem(lax.axis_index("band"), 2) * rows, 8)
    for side, out in enumerate((low, high)):
        for j in range(REACH):
            main, tail = pack_plane(orb[side, j].astype(F32))
            out[pl.ds(j * per_plane, n), :] = main
            out[pl.ds(j * per_plane + n, n // 2), :] = tail
            main, tail = pack_plane(pert[side, j])
            packed[pl.ds(j * per_plane, n), :] = main
            packed[pl.ds(j * per_plane + n, n // 2), :] = tail
        out[pl.ds(whole, rows), :] = packed[pl.ds(mine, rows), :]


def order_rows(n_band, share_ref, base_ref, part, tz):
    width, n = base_ref.shape[1:]
    wide = 2 * LANES
    for p in range(n_band):
        part[0, p * width:(p + 1) * width, :] = base_ref[share_ref[lax.axis_index("band"), p]]
    hi, lo = split(part[0])
    for k, cells in enumerate((hi, hi, lo)):
        tz[:, k * wide:k * wide + n] = cells
        tz[:, k * wide + n:(k + 1) * wide] = jnp.zeros((n, wide - n), BF16)


C_SRC, C_A, C_B, C_S, C_D0, C_G, C_P, C_T = 0, 1, 2, 3, 8, 9, 10, 11


def first_apply(co, d0, idx, pot, ccy_ref, cc_ref):
    centre = d0[idx]
    total = (co[C_A] - co[C_B] * pot) * centre + co[C_S] * lap_yz(centre, ccy_ref, cc_ref)
    for m in range(1, REACH + 1):
        total = total + (co[C_S] * (COEFFS[m] * DENOM)) * (d0[idx + m] + d0[idx - m])
    return total


def second_begin(co, d0, d1, idx, at, pot):
    centre = d1[idx, at]
    total = co[C_D0] * d0 + (co[C_G] - co[C_P] * pot) * centre
    for m in range(1, REACH + 1):
        total = total + (co[C_T] * (COEFFS[m] * DENOM)) * (d1[idx + m, at] + d1[idx - m, at])
    return centre, total


def first_kernel(n_band, share_ref, co, orb_hbm, pert_hbm, pot_hbm, cc_ref, ccy_ref, ty_ref, base_ref,
                 d1_hbm, send_ref, keep_ref, orb, d0, pot, d1, tz, lap, part, stack, freq, sem, out_sem):
    count_x = orb.shape[0]
    groups = count_x // REACH
    arrays = ((orb_hbm, orb), (pert_hbm, d0), (pot_hbm, pot))

    def copy(k, g):
        src, dst = arrays[k]
        where = pl.ds(g * REACH, REACH)
        return pltpu.make_async_copy(src.at[where], dst.at[where], sem.at[k, g])

    def copy_out(g):
        where = pl.ds(g * REACH, REACH)
        return pltpu.make_async_copy(d1.at[where], d1_hbm.at[where], out_sem.at[g])

    def source(g):
        for k in range(3):
            copy(k, g).wait()
        for j in range(REACH):
            x = g * REACH + j
            d0[x] = co[C_SRC] * (d0[x] * orb[x].astype(F32))

    for g in range(groups):
        for k in range(3):
            copy(k, g).start()
    order_rows(n_band, share_ref, base_ref, part, tz)
    source(0)
    source(1)

    def step(g, carry):
        source(g)
        for j in range(REACH):
            x = (g - 1) * REACH + j
            d1[x] = first_apply(co, d0, x, pot[x], ccy_ref, cc_ref)
        copy_out(g - 1).start()
        return carry

    lax.fori_loop(2, groups, step, 0)
    lead = 2 * REACH

    def begin(p, at):
        return second_begin(co, d0[lead + p, at], d1, lead + p, at, pot[lead + p, at])

    def finish(p, total, grad):
        return orb[lead + p].astype(F32) * (total + co[C_T] * grad)

    spectra(send_ref.shape[0], lambda t: None, begin, finish, ty_ref, tz, ccy_ref, cc_ref, (send_ref, keep_ref),
            lap, part, stack, freq)

    def done(g, carry):
        copy_out(g).wait()
        return carry

    lax.fori_loop(1, groups - 1, done, 0)


def inner_kernel(n_band, start, share_ref, co, orb_hbm, pert_hbm, pot_hbm, d1_hbm, cc_ref, ccy_ref, ty_ref, base_ref,
                 send_ref, keep_ref, orb, pert, pot, d1, tz, lap, part, stack, freq, sem, first_sem):
    pairs = send_ref.shape[0]
    lead = 2 * REACH
    arrays = (
        (orb_hbm, orb, start, 0), (pert_hbm, pert, start, 0), (pot_hbm, pot, start, 0),
        (d1_hbm, d1, start + REACH, lead),
    )

    def copy(k, i):
        src, dst, at, to = arrays[k]
        return pltpu.make_async_copy(src.at[pl.ds(at + 2 * i, 2)], dst.at[pl.ds(to + 2 * i, 2)], sem.at[k, i])

    ahead = pltpu.make_async_copy(d1_hbm.at[pl.ds(start - REACH, lead)], d1.at[pl.ds(0, lead)], first_sem.at[0])
    ahead.start()
    for i in range(pairs):
        for k in range(4):
            copy(k, i).start()
    order_rows(n_band, share_ref, base_ref, part, tz)
    ahead.wait()

    def before(t):
        for i in range(UNROLL // 2):
            for k in range(4):
                copy(k, UNROLL // 2 * t + i).wait()

    def begin(p, at):
        d0 = co[C_SRC] * (pert[p, at] * orb[p, at].astype(F32))
        return second_begin(co, d0, d1, p + REACH, at, pot[p, at])

    def finish(p, total, grad):
        return orb[p].astype(F32) * (total + co[C_T] * grad)

    spectra(pairs, before, begin, finish, ty_ref, tz, ccy_ref, cc_ref, (send_ref, keep_ref), lap, part, stack, freq)


def boundary_kernel(n_band, side, share_ref, co, orb_hbm, pert_hbm, pot_hbm, d1_hbm, mine, other,
                    cc_ref, ccy_ref, ty_ref, base_ref, send_ref, keep_ref,
                    orb, psi, pert, pot, d0, d1, packed, tz, lap, part, stack, freq, sem):
    count_x, n = orb_hbm.shape[0], orb_hbm.shape[1]
    per_plane = n + n // 2
    whole = REACH * per_plane
    span = 3 * REACH
    own = (0, count_x - 2 * REACH)[side]
    at_own = (REACH, 0)[side]
    halo = (0, 2 * REACH)[side]
    d1_own = (REACH, count_x - 3 * REACH)[side]
    d1_at = (3 * REACH, 0)[side]
    far = (0, 3 * REACH)[side]
    copies = [
        pltpu.make_async_copy(src.at[pl.ds(own, 2 * REACH)], dst.at[pl.ds(at_own, 2 * REACH)], sem.at[k])
        for k, (src, dst) in enumerate(((orb_hbm, orb), (pert_hbm, pert), (pot_hbm, pot)))
    ]
    copies.append(pltpu.make_async_copy(
        d1_hbm.at[pl.ds(d1_own, 2 * REACH)], d1.at[pl.ds(d1_at, 2 * REACH)], sem.at[3]))
    for c in copies:
        c.start()
    order_rows(n_band, share_ref, base_ref, part, tz)
    zero = jnp.zeros((n, n), F32)
    core = lax.rem(lax.axis_index("band"), 2)
    rows = whole // 2
    packed[pl.ds(pl.multiple_of(core * rows, 8), rows), :] = mine[pl.ds(whole, rows), :]
    packed[pl.ds(pl.multiple_of((1 - core) * rows, 8), rows), :] = other[...]
    for j in range(REACH):
        for src, dst in ((mine, psi), (packed, d0)):
            base = j * per_plane
            tail = src[pl.ds(base + n, n // 2), :]
            dst[halo + j, :, :LANES] = src[pl.ds(base, n), :]
            dst[halo + j, : n // 2, LANES:] = tail[:, : n - LANES]
            dst[halo + j, n // 2:, LANES:] = tail[:, n - LANES:]
        pot[halo + j] = zero
        d0[halo + j] = co[C_SRC] * (d0[halo + j] * psi[halo + j])
    for j in range(2 * REACH):
        d1[far + j] = zero
    for c in copies:
        c.wait()

    def fill(i, carry):
        wave = orb[at_own + i].astype(F32)
        psi[at_own + i] = wave
        d0[at_own + i] = co[C_SRC] * (pert[at_own + i] * wave)
        return carry

    lax.fori_loop(0, 2 * REACH, fill, 0)
    for j in range(REACH):
        d1[2 * REACH + j] = first_apply(co, d0, REACH + j, pot[REACH + j], ccy_ref, cc_ref)
    for j in range(REACH):
        d0[halo + j] = zero

    def begin(p, at):
        return second_begin(co, d0[p, at], d1, p + REACH, at, pot[p, at])

    def finish(p, total, grad):
        return psi[p] * (total + co[C_T] * grad)

    spectra(span // 2, lambda t: None, begin, finish, ty_ref, tz, ccy_ref, cc_ref, (send_ref, keep_ref),
            lap, part, stack, freq)


def pack_kernel(n_space, terms, share_ref, *refs):
    count = sum(terms)
    outs, cells = refs[count:-1], refs[-1]
    piece, size = outs[0].shape[0], outs[0].shape[1]
    width = refs[0].shape[2]
    half = width // 2
    slab = lax.axis_index("space")
    chunks = [refs[sum(terms[:c]):sum(terms[:c + 1])] for c in range(len(terms))]
    total = 2 * sum(chunk[0].shape[0] for chunk in chunks)
    if total < size or piece * n_space > 3 * half:
        cells[...] = jnp.zeros_like(cells)
    low = lax.broadcasted_iota(jnp.int32, (half, LANES), 1) < LANES // 2
    x = 0
    for chunk in chunks:
        for i in range(chunk[0].shape[0]):
            for j in range(2):
                cells[pl.ds(x + j, width, stride=size), :] = sum(ref[i, j] for ref in chunk[1:]) + chunk[0][i, j]
            tail = sum(ref[i, 2] for ref in chunk[1:]) + chunk[0][i, 2]
            a, b = tail[:half], tail[half:]
            cells[pl.ds(width * size + x, half, stride=size), :] = jnp.where(low, a, pltpu.roll(b, LANES // 2, 1))
            cells[pl.ds(width * size + x + 1, half, stride=size), :] = jnp.where(low, pltpu.roll(a, LANES // 2, 1), b)
            x += 2
    for k in range(n_space):
        dest = lax.rem(slab + k, n_space)
        for r in range(piece):
            where = pl.multiple_of((dest * piece + r) * size, 8)
            outs[k][r] = cells[pl.ds(where, size), :]


def x_kernel(n_space, batches, share_ref, *refs):
    ins = refs[:batches * n_space]
    ah_ref, al_ref, bh_ref, bl_ref, mul_ref = refs[batches * n_space:batches * n_space + 5]
    outs = refs[batches * n_space + 5:-2]
    cells, back = refs[-2:]
    slab = lax.axis_index("space")
    rows, size_out = outs[0].shape[0], outs[0].shape[1]
    parts = len(outs) // n_space
    total = sum(ins[i * n_space].shape[1] for i in range(batches))
    for k in range(n_space):
        at = lax.rem(slab - k + n_space, n_space) * total
        for i in range(batches):
            ref = ins[i * n_space + k]
            size = ref.shape[1]
            for r in range(rows):
                cells[pl.ds(pl.multiple_of(at, 8), size), r * LANES:(r + 1) * LANES] = ref[r]
            at = at + size
    spec = mm3(ah_ref[...], al_ref[...], cells[...]) * mul_ref[...]
    back[...] = mm3(bh_ref[...], bl_ref[...], spec)
    for k in range(n_space):
        for h in range(parts):
            at = pl.multiple_of((lax.rem(slab + k, n_space) * parts + h) * size_out, 8)
            for r in range(rows):
                outs[h * n_space + k][r] = back[pl.ds(at, size_out), r * LANES:(r + 1) * LANES]


def y_kernel(n_space, width, share_ref, *refs):
    ins = refs[:n_space]
    wh_ref, wl_ref = refs[n_space:n_space + 2]
    outs = refs[n_space + 2:-4]
    cells, rows_ref, prod, mixed = refs[-4:]
    piece, count_x = ins[0].shape[0], ins[0].shape[1]
    n_band = len(outs)
    half = width // 2
    per_tile = LANES // width
    tiles = outs[0].shape[0] // width
    me, slab = lax.axis_index("band"), lax.axis_index("space")
    for k in range(n_space):
        src = lax.rem(slab - k + n_space, n_space)
        for r in range(piece):
            where = pl.multiple_of((src * piece + r) * count_x, 8)
            cells[pl.ds(where, count_x), :] = ins[k][r]
    for i in range(per_tile):
        for t in range(tiles):
            x = t * per_tile + i
            at = (i * tiles + t) * width
            if x >= count_x:
                rows_ref[pl.ds(at, width), :] = jnp.zeros((width, 2 * LANES), F32)
                continue
            tail = cells[pl.ds(width * count_x + x, half, stride=count_x), :]
            rows_ref[pl.ds(at, width), :LANES] = cells[pl.ds(x, width, stride=count_x), :]
            rows_ref[pl.ds(at, half), LANES:] = tail
            rows_ref[pl.ds(at + half, half), LANES:] = pltpu.roll(tail, LANES // 2, 1)
    prod[...] = mm3_right(rows_ref[...], wh_ref[...], wl_ref[...])
    size = tiles * width
    lane = lax.broadcasted_iota(jnp.int32, (size, LANES), 1)
    for b in range(n_band):
        tile, spot = divmod(b, per_tile)
        acc = jnp.zeros((size, LANES), F32)
        for i in range(per_tile):
            part = prod[pl.ds(i * size, size), tile * LANES:(tile + 1) * LANES]
            shift = (i - spot) * width % LANES
            if shift:
                part = pltpu.roll(part, shift, 1)
            acc = jnp.where((lane >= i * width) & (lane < (i + 1) * width), part, acc)
        mixed[b ^ me] = acc
    for p in range(n_band):
        outs[p][...] = mixed[p]


def z_kernel(n_band, share_ref, *refs):
    th_ref, tl_ref, out_ref, stack = refs[-4:]
    ins = refs[:-4]
    parts = len(ins) // n_band
    count_x, width = out_ref.shape[0], out_ref.shape[1]
    size = count_x // parts
    per_tile = LANES // width
    tiles = ins[0].shape[0] // width
    for h in range(parts):
        for p in range(n_band):
            block = lax.axis_index("band") ^ p
            for t in range(tiles):
                stack[h * tiles + t, block] = ins[h * n_band + p][t * width:(t + 1) * width]
    for h in range(parts):
        for t in range(tiles):
            cells = stack[h * tiles + t].reshape(n_band * width, LANES)
            plane = mm3_right(cells.T, th_ref[...], tl_ref[...])
            for i in range(per_tile):
                x = t * per_tile + i
                if x < size:
                    out_ref[h * size + x] = plane[i * width:(i + 1) * width]


def shape_of(*dims, dtype=F32):
    return jax.ShapeDtypeStruct(dims, dtype)


def shift_perm(count, k):
    return [(i, (i + k) % count) for i in range(count)]


def coefficients(shift, occupation, total_orbitals):
    delta = 5.5
    theta = shift + delta
    ratio = theta / delta
    w0 = 1.0 / ratio
    w1 = 1.0 / (2.0 * ratio - w0)
    w2 = 1.0 / (2.0 * ratio - w1)
    b1 = 2.0 * w1 / delta
    b2 = 2.0 * w2 / delta
    weight = occupation * (4.0 / total_orbitals)
    centre = -0.5 * 3.0 * COEFFS[0]
    co = [jnp.zeros_like(shift)] * 16
    co[C_SRC] = -1.0 / theta
    co[C_A] = w1 * w0 + b1 * theta - b1 * (shift + centre)
    co[C_B] = b1
    co[C_S] = 0.5 * b1 / DENOM
    co[C_D0] = weight * (1.0 - w2 * w0)
    co[C_G] = weight * (1.0 + w2 * w1 + w2 / w1 - b2 * (shift + centre))
    co[C_P] = weight * b2
    co[C_T] = weight * 0.5 * b2 / DENOM
    return jnp.stack(co)


def chunk_sizes(groups):
    first = -(-groups // 2)
    return [first, groups - first]


def ceil8(count):
    return -(-count // 8) * 8


def program_on_device(orbitals, occupations, shifts, perturbations, local_potential):
    count_x, n = orbitals.shape[1], orbitals.shape[2]
    n_band, n_space = lax.axis_size("band"), lax.axis_size("space")
    bits = n_band.bit_length() - 1
    assert orbitals.shape[0] == 1 and perturbations.shape[0] == 1 and n_band == 1 << bits
    assert 2 * (n - LANES) == LANES and count_x % 8 == 0 and count_x >= 5 * REACH
    band, slab = lax.axis_index("band"), lax.axis_index("space")
    orders = block_orders(n_band)
    share = jnp.asarray(orders)
    orb, pert, pot = orbitals[0], perturbations[0], local_potential
    width = n // n_band
    half = width // 2
    per_plane = n + n // 2
    wide = 2 * LANES
    smem = pl.BlockSpec(memory_space=pltpu.SMEM)
    vmem = pl.BlockSpec(memory_space=pltpu.VMEM)
    anywhere = pl.BlockSpec(memory_space=pl.ANY)
    dma = pltpu.SemaphoreType.DMA
    co = coefficients(shifts[0], occupations[0], n_band * orbitals.shape[0])

    base = cas_np(range(n), range(n), n)
    base_h, base_l = split_np(base)
    ring = circulant_np(n)
    ring_y = np.concatenate([ring, ring], axis=1)
    ty = np.concatenate([base_h, base_h, base_l], axis=1)
    whole = REACH * per_plane
    low, high = pl.pallas_call(
        edges_kernel,
        out_shape=[shape_of(whole + whole // 2, LANES)] * 2,
        in_specs=[smem, anywhere, anywhere],
        out_specs=[vmem] * 2,
        scratch_shapes=[
            pltpu.VMEM((2, REACH, n, n), BF16), pltpu.VMEM((2, REACH, n, n), F32),
            pltpu.VMEM((whole, LANES), F32), dma((2, 2)),
        ],
        name="edges", compiler_params=pltpu.CompilerParams(vmem_limit_bytes=MOST),
    )(share, orb, pert)
    cores = [(b, b ^ 1) for b in range(n_band)]
    halos = []
    for cells, k in ((high, 1), (low, n_space - 1)):
        mine = lax.ppermute(cells, "space", shift_perm(n_space, k))
        other = lax.ppermute(mine[whole:], "band", cores)
        halos.append((mine, other))

    tables = (jnp.asarray(ring), jnp.asarray(ring_y), jnp.asarray(ty), jnp.asarray(base.reshape(n_band, width, n)))
    table_specs = [vmem] * 4

    def halves(pairs):
        return [shape_of(pairs, 3, n // 2, LANES)] * 2

    def stages():
        return [
            pltpu.VMEM((n, 3 * wide), BF16), pltpu.VMEM((UNROLL, 2 * n, n), BF16), pltpu.VMEM((UNROLL, n, n), F32),
            pltpu.VMEM((UNROLL, 3 * n, n), BF16), pltpu.VMEM((UNROLL, n, 3 * wide), BF16),
        ]

    chunks = chunk_sizes(count_x // REACH - 4)
    size_a = chunks[0] * REACH
    d1, *sent_a = pl.pallas_call(
        lambda *refs: first_kernel(n_band, *refs),
        out_shape=[shape_of(count_x, n, n)] + halves(size_a // 2),
        in_specs=[smem, smem] + [anywhere] * 3 + table_specs,
        out_specs=[anywhere, vmem, vmem],
        scratch_shapes=[
            pltpu.VMEM((count_x, n, n), BF16), pltpu.VMEM((count_x, n, n), F32),
            pltpu.VMEM((count_x, n, n), F32), pltpu.VMEM((count_x, n, n), F32), *stages(),
            dma((3, count_x // REACH)), dma((count_x // REACH,)),
        ],
        name="first_a", compiler_params=pltpu.CompilerParams(vmem_limit_bytes=MOST),
    )(share, co, orb, pert, pot, *tables)

    def inner(start, count):
        return pl.pallas_call(
            lambda *refs: inner_kernel(n_band, start, *refs),
            out_shape=halves(count // 2),
            in_specs=[smem, smem] + [anywhere] * 4 + table_specs,
            out_specs=[vmem, vmem],
            scratch_shapes=[
                pltpu.VMEM((count, n, n), BF16), pltpu.VMEM((count, n, n), F32), pltpu.VMEM((count, n, n), F32),
                pltpu.VMEM((count + 2 * REACH, n, n), F32), *stages(), dma((4, count // 2)), dma((1,)),
            ],
            compiler_params=pltpu.CompilerParams(vmem_limit_bytes=50 * MIB),
        )(share, co, orb, pert, pot, d1, *tables)

    span = 3 * REACH

    def outer(side, halo):
        return pl.pallas_call(
            lambda *refs: boundary_kernel(n_band, side, *refs),
            out_shape=halves(span // 2),
            in_specs=[smem, smem] + [anywhere] * 4 + [vmem] * 2 + table_specs,
            out_specs=[vmem, vmem],
            scratch_shapes=[
                pltpu.VMEM((span, n, n), BF16), pltpu.VMEM((span, n, n), F32), pltpu.VMEM((span, n, n), F32),
                pltpu.VMEM((span, n, n), F32), pltpu.VMEM((span, n, n), F32), pltpu.VMEM((5 * REACH, n, n), F32),
                pltpu.VMEM((whole, LANES), F32), *stages(), dma((4,)),
            ],
            compiler_params=pltpu.CompilerParams(vmem_limit_bytes=46 * MIB),
        )(share, co, orb, pert, pot, d1, *halo, *tables)

    def halving(send, keep):
        for stage in range(bits):
            perm = [(b, partner(b, stage, bits)) for b in range(n_band)]
            got = lax.ppermute(send, "band", perm)
            if stage < bits - 1:
                cut = keep.shape[2] // 2
                send, keep = keep[:, :, :cut] + got[:, :, :cut], keep[:, :, cut:] + got[:, :, cut:]
        return [keep, got]

    def direct(send, keep):
        perm = [(b, partner(b, 0, bits)) for b in range(n_band)]
        got = lax.ppermute(send, "band", perm)
        blocks = []
        for m in range(n_band // 2):
            rows = slice(m * width, (m + 1) * width)
            block = keep[:, :, rows] + got[:, :, rows]
            if m < n_band // 2 - 1:
                perm = [(b, int(orders[b, n_band // 2 + m])) for b in range(n_band)]
                block = lax.ppermute(block, "band", perm)
            blocks.append(block)
        return blocks

    piece = -(-3 * half // n_space)

    def to_columns(chunks):
        size = ceil8(2 * sum(chunk[0].shape[0] for chunk in chunks))
        blocks = pl.pallas_call(
            lambda *refs: pack_kernel(n_space, [len(chunk) for chunk in chunks], *refs),
            out_shape=[shape_of(piece, size, LANES)] * n_space,
            in_specs=[smem] + [vmem] * sum(len(chunk) for chunk in chunks),
            out_specs=[vmem] * n_space,
            scratch_shapes=[pltpu.VMEM((piece * n_space * size, LANES), F32)],
            compiler_params=pltpu.CompilerParams(vmem_limit_bytes=12 * MIB),
        )(share, *(ref for chunk in chunks for ref in chunk))
        return [lax.ppermute(blocks[k], "space", shift_perm(n_space, k)) if k else blocks[0] for k in range(n_space)]

    inside = np.arange(2 * REACH, count_x - 2 * REACH)
    planes = {
        "a": inside[:size_a],
        "b": inside[size_a:],
        "p": np.arange(-REACH, 2 * REACH),
        "q": np.arange(count_x - 2 * REACH, count_x + REACH),
    }
    sums = [
        direct(*sent_a),
        direct(*inner(2 * REACH + size_a, chunks[1] * REACH)),
        halving(*outer(0, halos[0])),
        halving(*outer(1, halos[1])),
    ]
    batches = (("a", "b"), ("p", "q"))
    at = dict(zip(planes, sums))
    received = [to_columns([at[name] for name in names]) for names in batches]

    a_parts = []
    for s in range(n_space):
        for names in batches:
            at = np.concatenate([planes[name] for name in names])
            block = base[:, (s * count_x + at) % n]
            a_parts.append(np.pad(block, ((0, 0), (0, ceil8(len(at)) - len(at)))))
    a_h, a_l = split_np(np.concatenate(a_parts, axis=1))

    def folded(values):
        return jnp.minimum(values, n - values).astype(F32)

    row = slab * piece + jnp.arange(piece, dtype=jnp.int32)[:, None]
    lane = jnp.arange(LANES, dtype=jnp.int32)[None, :]
    is_tail = row >= width
    ky = jnp.where(is_tail, LANES + lane % (LANES // 2), lane)
    kz_in = jnp.where(is_tail, row - width + jnp.where(lane < LANES // 2, 0, half), row)
    kz = jnp.clip(band * width + kz_in, 0, n)
    squares = (folded(ky) ** 2 + folded(kz) ** 2).reshape(1, piece * LANES)
    kx = folded(jnp.arange(n, dtype=jnp.int32))
    multiplier = (256.0 / float(n) ** 3) / jnp.sqrt(squares + (kx ** 2)[:, None] + 1.0)

    n_parts = 1
    part_x = count_x // n_parts
    base_h, base_l = jnp.asarray(base_h), jnp.asarray(base_l)
    backs = pl.pallas_call(
        lambda *refs: x_kernel(n_space, len(received), *refs),
        out_shape=[shape_of(piece, part_x, LANES)] * (n_space * n_parts),
        in_specs=[smem] + [vmem] * (len(received) * n_space + 5),
        out_specs=[vmem] * (n_space * n_parts),
        scratch_shapes=[
            pltpu.VMEM((a_h.shape[1], piece * LANES), F32), pltpu.VMEM((n, piece * LANES), F32),
        ],
        name="along_x", compiler_params=pltpu.CompilerParams(vmem_limit_bytes=20 * MIB),
    )(share, *(ref for blocks in received for ref in blocks), jnp.asarray(a_h), jnp.asarray(a_l), base_h, base_l, multiplier)
    per_tile = LANES // width
    tiles = -(-part_x // per_tile)
    y_tiles = -(-n_band // per_tile)
    w_table = np.zeros((wide, y_tiles * LANES), np.float32)
    for b in range(n_band):
        t, spot = divmod(b, per_tile)
        w_table[:n, t * LANES + spot * width:t * LANES + (spot + 1) * width] = base[:, b * width:(b + 1) * width]
    w_h, w_l = split_np(w_table)
    rows_y = per_tile * tiles * width
    pieces = []
    for h in range(n_parts):
        blocks = backs[h * n_space:(h + 1) * n_space]
        slabs = [lax.ppermute(blocks[k], "space", shift_perm(n_space, k)) if k else blocks[0] for k in range(n_space)]
        by_rows = pl.pallas_call(
            lambda *refs: y_kernel(n_space, width, *refs),
            out_shape=[shape_of(tiles * width, LANES)] * n_band,
            in_specs=[smem] + [vmem] * (n_space + 2),
            out_specs=[vmem] * n_band,
            scratch_shapes=[
                pltpu.VMEM((piece * n_space * part_x, LANES), F32),
                pltpu.VMEM((rows_y, wide), F32),
                pltpu.VMEM((rows_y, y_tiles * LANES), F32),
                pltpu.VMEM((n_band, tiles * width, LANES), F32),
            ],
            compiler_params=pltpu.CompilerParams(vmem_limit_bytes=24 * MIB),
        )(share, *slabs, jnp.asarray(w_h), jnp.asarray(w_l))
        pieces += [
            lax.ppermute(by_rows[p], "band", [(b, b ^ p) for b in range(n_band)])
            if p else by_rows[0]
            for p in range(n_band)
        ]

    out = pl.pallas_call(
        lambda *refs: z_kernel(n_band, *refs),
        out_shape=shape_of(count_x, width, n),
        in_specs=[smem] + [vmem] * (n_parts * n_band + 2),
        out_specs=vmem,
        scratch_shapes=[pltpu.VMEM((n_parts * tiles, n_band, width, LANES), F32)],
        name="along_z", compiler_params=pltpu.CompilerParams(vmem_limit_bytes=16 * MIB),
    )(share, *pieces, base_h, base_l)
    return out[None]


def solution(mesh):
    in_specs = (
        P("band", "space", None, None),
        P("band"),
        P("band"),
        P(None, "space", None, None),
        P("space", None, None),
    )
    out_specs = P(None, "space", "band", None)
    return jax.shard_map(program_on_device, mesh=mesh, in_specs=in_specs, out_specs=out_specs, check_vma=False)
```
